128 devices in a mesh: row: 16 (over y_hi, x, core), col: 8 (over z, y_lo).
Axes of the slice: x: 4, y: 4 (y_hi: 2, y_lo: 2; y = y_hi * 2 + y_lo), z: 4, core: 2. Of those that a mesh axis runs over, the one named last changes fastest.
Arguments:
- first_view: bfloat16 [512, 16384], P(None, 'row'), may hold values from -20 to 20
- second_view: bfloat16 [512, 16384], P(None, 'row'), may hold values from -20 to 20
- projector: bfloat16 [16384, 16384], P('row', 'col'), may hold values from -1 to 1
Outputs:
- grad_first: float32 [512, 8, 16, 128], P(None, 'col', 'row')
- grad_second: float32 [512, 8, 16, 128], P(None, 'col', 'row')
- correlation: float32 [8, 16, 128, 16384], P(None, 'row', None, 'col')
The draws below stay inside these ranges and needn't reach their ends.
All inputs are finite; a program needn't handle non-finite values.
Results may differ from the reference program's by a relative error of at most 0.0003.
Values sent between devices are 32-bit elements; how exact they have to be, the bound alone decides.
No kernel may reach another device: no remote copies, remote signals or barrier semaphores. Data moves between devices by JAX's collectives and lax.ppermute only.
A program may use at most 128 MiB of HBM per device.

```python
import math
import jax
import jax.numpy as jnp
from jax import lax

BATCH = 512
PROJ = 16384
N_ROW = 16
N_COL = 8


def draw_first_view(key, part):
    key = jax.random.fold_in(key, 11)
    key_base, key_mean = jax.random.split(key, 2)
    means = jax.random.uniform(key_mean, (1, PROJ), jnp.float32, -1.0, 1.0)
    base = jax.random.truncated_normal(key_base, -4.0, 4.0, (BATCH, PROJ), jnp.float32)
    return (base + means).astype(jnp.bfloat16)


def draw_second_view(key, part):
    key = jax.random.fold_in(key, 12)
    key_base, key_mean = jax.random.split(key, 2)
    means = jax.random.uniform(key_mean, (1, PROJ), jnp.float32, -1.0, 1.0)
    base = jax.random.truncated_normal(key_base, -4.0, 4.0, (BATCH, PROJ), jnp.float32)
    return (base + means).astype(jnp.bfloat16)


def draw_projector(key, part):
    key = jax.random.fold_in(key, 13)
    key_base, key_scale = jax.random.split(key, 2)
    base = jax.random.truncated_normal(key_base, -4.0, 4.0, (PROJ, PROJ), jnp.float32)
    scales = jnp.exp(jax.random.uniform(key_scale, (1, PROJ), jnp.float32, 0.0, math.log(10.0)))
    return (base * scales / math.sqrt(PROJ)).astype(jnp.bfloat16)


def setup_inputs(seed: int = 0) -> dict:
    key_list = jax.random.split(jax.random.key(seed), 4)
    first_view = draw_first_view(jax.random.fold_in(key_list[3], 71), 0)
    second_view = draw_second_view(jax.random.fold_in(key_list[3], 71), 0)
    projector = draw_projector(jax.random.fold_in(key_list[3], 71), 0)
    return {"first_view": first_view, "second_view": second_view, "projector": projector}


off_weight = 0.0051
epsilon = 1e-05

def standardize(values):
    average = lax.optimization_barrier(jnp.mean(values, axis=0, keepdims=True))
    centred = values - average
    spread = lax.optimization_barrier(jnp.mean(centred * centred, axis=0, keepdims=True))
    return centred * lax.rsqrt(spread + epsilon)

def reference(first_view, second_view, projector):
    first_std = standardize(jnp.dot(first_view, projector, preferred_element_type=jnp.float32))
    second_std = standardize(jnp.dot(second_view, projector, preferred_element_type=jnp.float32))
    clip_count = first_std.shape[0]
    blocks = 16
    stride = PROJ // blocks
    first_blocks = first_std.reshape(clip_count, blocks, stride).transpose(1, 0, 2)
    identity = jnp.eye(stride, dtype=jnp.float32)
    highest = lax.Precision.HIGHEST

    def step(carry, inputs):
        index, first_part = inputs
        correlation = jnp.dot(first_part.T, second_std, precision=highest, preferred_element_type=jnp.float32) / clip_count
        offset = (index * stride).astype(jnp.int32)
        zero = jnp.zeros((), jnp.int32)
        diag_block = lax.dynamic_slice(correlation, (zero, offset), (stride, stride))
        coupling = lax.dynamic_update_slice(2.0 * off_weight * correlation, 2.0 * off_weight * diag_block + identity * ((2.0 - 2.0 * off_weight) * diag_block - 2.0), (zero, offset))
        grad_part = jnp.dot(second_std, coupling.T, precision=highest, preferred_element_type=jnp.float32)
        carry = carry + jnp.dot(first_part, coupling, precision=highest, preferred_element_type=jnp.float32)
        return (carry, (grad_part, correlation))
    start_carry = jnp.zeros((clip_count, PROJ), jnp.float32)
    grad_two, (parts, corr_parts) = lax.scan(step, start_carry, (jnp.arange(blocks, dtype=jnp.int32), first_blocks))
    grad_one = parts.transpose(1, 0, 2).reshape(clip_count, PROJ)
    shard = PROJ // (N_ROW * N_COL)
    out_shape = (clip_count, N_COL, N_ROW, shard)
    corr_full = corr_parts.reshape(N_COL, N_ROW, shard, PROJ)
    return (grad_one.reshape(out_shape), grad_two.reshape(out_shape), corr_full)
```

```python
import jax
import jax.numpy as jnp
from jax import lax
from jax.sharding import PartitionSpec as P

off_weight = 0.0051
epsilon = 1e-05


def product(left, right, contract, precision=lax.Precision.HIGH):
    return lax.dot_general(
        left, right, (contract, ((), ())), precision=precision, preferred_element_type=jnp.float32
    )


def standardize(values):
    average = jnp.mean(values, axis=0, keepdims=True)
    centred = values - average
    spread = jnp.mean(centred * centred, axis=0, keepdims=True)
    return centred * lax.rsqrt(spread + epsilon)


def shards(first_view, second_view, projector):
    clip_count = first_view.shape[0]
    rows = lax.axis_size("row")
    col_width = projector.shape[1]
    stride = col_width // rows

    def partial(view):
        sums = lax.dot_general(
            view, projector, (((1,), (0,)), ((), ())), preferred_element_type=jnp.float32
        )
        return sums.reshape(clip_count, rows, stride).transpose(1, 0, 2)

    projected = lax.psum_scatter(
        jnp.concatenate((partial(first_view), partial(second_view)), axis=1),
        "row",
        scatter_dimension=0,
        tiled=True,
    )
    first_std = standardize(projected[0, :clip_count])
    second_std = standardize(projected[0, clip_count:])
    grams = lax.psum(
        jnp.stack(
            (
                product(first_std, first_std, ((1,), (1,))),
                product(second_std, second_std, ((1,), (1,))),
            )
        ),
        ("row", "col"),
    )
    second_block = lax.all_gather(second_std, "row", axis=0)
    first_block = lax.all_gather(first_std, "col", axis=0)
    correlation = product(first_block, second_block, ((1,), (1,))) / clip_count
    corr_out = correlation.reshape(first_block.shape[0], 1, stride, col_width)
    diagonal = (2.0 - 2.0 * off_weight) * jnp.mean(first_std * second_std, axis=0, keepdims=True) - 2.0
    scale = 2.0 * off_weight / clip_count
    grad_one = scale * product(grams[1], first_std, ((1,), (0,))) + second_std * diagonal
    grad_two = scale * product(grams[0], second_std, ((1,), (0,))) + first_std * diagonal
    return (
        grad_one.reshape(clip_count, 1, 1, stride),
        grad_two.reshape(clip_count, 1, 1, stride),
        corr_out,
    )


def solution(mesh):
    in_specs = (P(None, "row"), P(None, "row"), P("row", "col"))
    out_specs = (
        P(None, "col", "row", None),
        P(None, "col", "row", None),
        P(None, "row", None, "col"),
    )
    return jax.shard_map(shards, mesh=mesh, in_specs=in_specs, out_specs=out_specs, check_vma=False)
```

```python
import functools

import jax
import jax.numpy as jnp
import numpy as np
from jax import lax
from jax.experimental import pallas as pl
from jax.experimental.pallas import tpu as pltpu
from jax.sharding import PartitionSpec as P

off_weight = 0.0051
epsilon = 1e-05
BOTH = ("row", "col")
F32 = jnp.float32
BF16 = jnp.bfloat16


def place(index):
    row, col = divmod(index, 8)
    return row // 8, row // 2 % 4, row % 2, col // 2, col % 2


def index_of(y_hi, x, core, z, y_lo):
    return (y_hi * 8 + x % 4 * 2 + core) * 8 + z % 4 * 2 + y_lo


def first_mate(x):
    return x ^ 1


def second_mate(x):
    return (3, 2, 1, 0)[x]


def hop(values, move):
    pairs = [(i, index_of(*move(*place(i)))) for i in range(128)]
    return lax.ppermute(values, BOTH, pairs)


def to_core(v):
    return hop(v, lambda h, x, k, z, l: (h, x, 1 - k, z, l))


def to_first(v):
    return hop(v, lambda h, x, k, z, l: (h, first_mate(x), k, z, l))


def to_second(v):
    return hop(v, lambda h, x, k, z, l: (h, second_mate(x), k, z, l))


def to_far(v):
    return hop(v, lambda h, x, k, z, l: (1 - h, x, k, z, l))


def to_near(v):
    return hop(v, lambda h, x, k, z, l: (h, x, k, z, 1 - l))


def along_x(v, step):
    return hop(v, lambda h, x, k, z, l: (h, x + step, k, z, l))


def along_z(v, step):
    return hop(v, lambda h, x, k, z, l: (h, x, k, z + step, l))


def tables():
    rows = []
    for i in range(128):
        h, x, k, z, l = place(i)
        own, one, two, opp = x, first_mate(x), second_mate(x), (x + 2) % 4
        blocks = lambda half, order: [half * 4 + b for b in order]
        first = blocks(h, (own, two, one, opp)) + blocks(1 - h, (own, one, two, opp))
        second = blocks(h, (own, one, two, opp)) + blocks(1 - h, (own, one, two, opp))
        gathered = [half * 4 + (x + s) % 4 for s in (0, -1, 1, 2) for half in (h, 1 - h)]
        columns = [(z + s) % 4 * 2 + low for s in (0, -1, 1, 2) for low in (l, 1 - l)]
        rows.append(first + second + gathered + columns + [k] + [0] * 7)
    return np.asarray(rows, np.int32)


FIRST, SECOND, GATHERED, COLUMNS, CORE = 0, 8, 16, 24, 32


def split(value):
    high = value.astype(BF16)
    return high, (value - high.astype(F32)).astype(BF16)


def dot(a, b, dims):
    return lax.dot_general(a, b, (dims, ((), ())), preferred_element_type=F32)


def dot3(a, b, dims):
    return dot(a[0], b[0], dims) + (dot(a[0], b[1], dims) + dot(a[1], b[0], dims))


PARAMS = dict(vmem_limit_bytes=56 * 1024 * 1024)


def project(table, view, projector, offset):
    clips, depth = view.shape
    blocks = projector.shape[1] // 256

    def body(table_ref, view_ref, weight_ref, send_ref, keep_ref):
        sums = dot(view_ref[...], weight_ref[...], ((1,), (0,)))
        low, high = sums[:, :128], sums[:, 128:]
        is_low = table_ref[CORE] == 0
        send_ref[0] = jnp.where(is_low, high, low)
        keep_ref[0] = jnp.where(is_low, low, high)

    piece = pl.BlockSpec((1, clips, 128), lambda j, t: (j, 0, 0))
    return pl.pallas_call(
        body,
        out_shape=[jax.ShapeDtypeStruct((blocks, clips, 128), F32)] * 2,
        grid_spec=pltpu.PrefetchScalarGridSpec(
            num_scalar_prefetch=1,
            grid=(blocks,),
            in_specs=[
                pl.BlockSpec((clips, depth), lambda j, t: (0, 0)),
                pl.BlockSpec((depth, 256), lambda j, t: (0, t[offset + j])),
            ],
            out_specs=[piece, piece],
        ),
        compiler_params=pltpu.CompilerParams(**PARAMS),
        cost_estimate=pl.CostEstimate(
            flops=2 * clips * depth * blocks * 256, bytes_accessed=14 << 20, transcendentals=0
        ),
        name="project",
    )(table, view, projector)


def standardize_rows(values):
    average = jnp.mean(values, axis=0, keepdims=True)
    centred = values - average
    spread = jnp.mean(centred * centred, axis=0, keepdims=True)
    return centred * lax.rsqrt(spread + epsilon)


def standardize(whole, top=(), bottom=()):
    clips = whole[0].shape[1]
    half = clips // 2

    def body(*refs):
        ins, out_ref = refs[:-1], refs[-1]
        whole_refs, halves = ins[: len(whole)], ins[len(whole) :]
        total = sum(ref[0] for ref in whole_refs)
        if halves:
            upper = sum(ref[0] for ref in halves[: len(top)])
            lower = sum(ref[0] for ref in halves[len(top) :])
            total = total + jnp.concatenate((upper, lower), axis=0)
        out_ref[0] = standardize_rows(total)

    spec = lambda rows: pl.BlockSpec((1, rows, 128), lambda j: (0, 0, 0))
    return pl.pallas_call(
        body,
        grid=(1,),
        out_shape=jax.ShapeDtypeStruct((1, clips, 128), F32),
        in_specs=[spec(clips)] * len(whole) + [spec(half)] * (len(top) + len(bottom)),
        out_specs=spec(clips),
        compiler_params=pltpu.CompilerParams(**PARAMS),
        name="standardize",
    )(*whole, *top, *bottom)


def prepare(table, pieces):
    clips = pieces[0].shape[1]

    def body(table_ref, *refs):
        ins, outs = refs[:4], refs[4:]
        turned_high, turned_low, high_ref, low_ref, gram_ref, total = outs
        for j in range(8):
            value = ins[j // 2][j % 2]
            high, low = split(value)
            spot = table_ref[COLUMNS + j]
            high_ref[spot] = high
            low_ref[spot] = low
            flipped = split(value.T)
            turned_high[spot] = flipped[0]
            turned_low[spot] = flipped[1]
            term = dot3((high, low), flipped, ((1,), (0,)))
            if j == 0:
                total[...] = term
            else:
                total[...] += term
        gram_ref[...] = total[pl.ds(pl.multiple_of(table_ref[COLUMNS] * (clips // 8), clips // 8), clips // 8), :]

    pair = lambda: pl.BlockSpec((2, clips, 128), lambda j, t: (0, 0, 0))
    return pl.pallas_call(
        body,
        out_shape=[
            jax.ShapeDtypeStruct((8, 128, clips), BF16),
            jax.ShapeDtypeStruct((8, 128, clips), BF16),
            jax.ShapeDtypeStruct((8, clips, 128), BF16),
            jax.ShapeDtypeStruct((8, clips, 128), BF16),
            jax.ShapeDtypeStruct((clips // 8, clips), F32),
        ],
        grid_spec=pltpu.PrefetchScalarGridSpec(
            num_scalar_prefetch=1,
            grid=(1,),
            in_specs=[pair() for _ in range(4)],
            out_specs=[
                pl.BlockSpec((8, 128, clips), lambda j, t: (0, 0, 0)),
                pl.BlockSpec((8, 128, clips), lambda j, t: (0, 0, 0)),
                pl.BlockSpec((8, clips, 128), lambda j, t: (0, 0, 0)),
                pl.BlockSpec((8, clips, 128), lambda j, t: (0, 0, 0)),
                pl.BlockSpec((clips // 8, clips), lambda j, t: (0, 0)),
            ],
            scratch_shapes=[pltpu.VMEM((clips, clips), F32)],
        ),
        compiler_params=pltpu.CompilerParams(**PARAMS),
        cost_estimate=pl.CostEstimate(
            flops=6 * clips * clips * 1024, bytes_accessed=7 << 20, transcendentals=0
        ),
        name="prepare",
    )(table, *pieces)


def spread_gradient(mine, theirs, high, low):
    clips = mine[0].shape[1]

    def body(*refs):
        own_refs, other_refs = refs[:4], refs[4:8]
        high_ref, low_ref, out_ref, total = refs[8:]
        for j in range(8):
            value = jnp.concatenate((own_refs[j // 2][j % 2], other_refs[j // 2][j % 2]), axis=1)
            parts = split(value)
            term = dot3(parts, parts, ((1,), (1,)))
            if j == 0:
                total[...] = term
            else:
                total[...] += term
        gram = split(total[...])
        for j in range(8):
            out_ref[j] = dot3(gram, (high_ref[j], low_ref[j]), ((1,), (0,)))

    pair = lambda: pl.BlockSpec((2, clips, 128), lambda j: (0, 0, 0))
    full = lambda: pl.BlockSpec((8, clips, 128), lambda j: (0, 0, 0))
    return pl.pallas_call(
        body,
        grid=(1,),
        out_shape=jax.ShapeDtypeStruct((8, clips, 128), F32),
        in_specs=[pair() for _ in range(8)] + [full(), full()],
        out_specs=full(),
        scratch_shapes=[pltpu.VMEM((clips, clips), F32)],
        compiler_params=pltpu.CompilerParams(**PARAMS),
        cost_estimate=pl.CostEstimate(
            flops=6 * clips * clips * 3072, bytes_accessed=8 << 20, transcendentals=0
        ),
        name="spread_gradient",
    )(*mine, *theirs, high, low)


def correlate(table, mine, theirs, turned_high, turned_low):
    clips = mine[0].shape[1]

    def body(table_ref, *refs):
        own_refs, other_refs = refs[:4], refs[4:8]
        high_ref, low_ref, out_ref = refs[8:]
        step = pl.program_id(0)
        is_low = table_ref[CORE] == 0
        left = (high_ref[...].reshape(1024, clips), low_ref[...].reshape(1024, clips))
        for group in range(4):

            @pl.when(step // 2 == group)
            def _():
                own, other = own_refs[group][0], other_refs[group][0]
                value = jnp.concatenate(
                    (jnp.where(is_low, own, other), jnp.where(is_low, other, own)), axis=1
                )
                found = dot3(left, split(value), ((1,), (0,))) * (1.0 / clips)
                out_ref[...] = found.reshape(8, 1, 128, 256)

    def pick(group):
        return pl.BlockSpec((1, clips, 128), lambda j, t: (jnp.clip(j - 2 * group, 0, 1), 0, 0))

    full = lambda: pl.BlockSpec((8, 128, clips), lambda j, t: (0, 0, 0))
    return pl.pallas_call(
        body,
        out_shape=jax.ShapeDtypeStruct((8, 1, 128, 2048), F32),
        grid_spec=pltpu.PrefetchScalarGridSpec(
            num_scalar_prefetch=1,
            grid=(8,),
            in_specs=[pick(g) for g in range(4)] * 2 + [full(), full()],
            out_specs=pl.BlockSpec((8, 1, 128, 256), lambda j, t: (0, 0, 0, t[GATHERED + j])),
        ),
        compiler_params=pltpu.CompilerParams(**PARAMS),
        cost_estimate=pl.CostEstimate(
            flops=6 * clips * 1024 * 2048, bytes_accessed=14 << 20, transcendentals=0
        ),
        name="correlate",
    )(table, *mine, *theirs, turned_high, turned_low)


def finish_second(table, rows, first_std, second_std):
    clips = second_std.shape[1]
    slab = clips // 8

    def body(table_ref, *refs):
        ins, (first_ref, second_ref, out_ref) = refs[:4], refs[4:]
        first, second = first_ref[0], second_ref[0]
        diagonal = (2.0 - 2.0 * off_weight) * jnp.mean(first * second, axis=0, keepdims=True) - 2.0
        right = split(second)
        for j in range(8):
            found = dot3(split(ins[j // 2][j % 2]), right, ((1,), (0,)))
            at = pl.ds(pl.multiple_of(table_ref[COLUMNS + j] * slab, slab), slab)
            out_ref[at, :] = (2.0 * off_weight / clips) * found + first_ref[0, at, :] * diagonal

    piece = lambda: pl.BlockSpec((1, clips, 128), lambda j, t: (0, 0, 0))
    return pl.pallas_call(
        body,
        out_shape=jax.ShapeDtypeStruct((clips, 128), F32),
        grid_spec=pltpu.PrefetchScalarGridSpec(
            num_scalar_prefetch=1,
            grid=(1,),
            in_specs=[pl.BlockSpec((2, slab, clips), lambda j, t: (0, 0, 0)) for _ in range(4)]
            + [piece(), piece()],
            out_specs=pl.BlockSpec((clips, 128), lambda j, t: (0, 0)),
        ),
        compiler_params=pltpu.CompilerParams(**PARAMS),
        name="finish_second",
    )(table, *rows, first_std, second_std)


def finish_first(parts, first_std, second_std):
    clips = second_std.shape[1]

    def body(parts_ref, first_ref, second_ref, out_ref):
        first, second = first_ref[0], second_ref[0]
        diagonal = (2.0 - 2.0 * off_weight) * jnp.mean(first * second, axis=0, keepdims=True) - 2.0
        total = sum(parts_ref[j] for j in range(8))
        out_ref[...] = (2.0 * off_weight / clips) * total + second * diagonal

    return pl.pallas_call(
        body,
        out_shape=jax.ShapeDtypeStruct((clips, 128), F32),
        compiler_params=pltpu.CompilerParams(**PARAMS),
        name="finish_first",
    )(parts, first_std, second_std)


def reduce_first(send, keep):
    got = to_core(send)
    have = lambda a, b: keep[a:b] + got[a:b]
    one = to_first(have(2, 4))
    two = to_second(have(6, 8))
    one_more = to_second(have(1, 2) + one[1:])
    two_more = to_first(have(5, 6) + two[1:])
    far = to_far(have(4, 5) + two[:1] + two_more)
    return standardize([keep, got, one, one_more, far])


def reduce_second(send, keep):
    got = to_core(send)
    far = to_far(keep[4:] + got[4:])
    half = send.shape[1] // 2
    have = lambda i, rows: keep[i : i + 1, rows] + got[i : i + 1, rows] + far[i : i + 1, rows]
    top, bottom = slice(0, half), slice(half, 2 * half)
    one = to_first(jnp.concatenate((have(1, top), have(3, top)), axis=0))
    two = to_second(jnp.concatenate((have(2, bottom), have(3, bottom)), axis=0))
    one_more = to_second(have(2, top) + one[1:])
    two_more = to_first(have(1, bottom) + two[1:])
    return standardize([keep, got, far], [one, one_more], [two, two_more])


def fan(values, along):
    return [values, along(values, 1), along(values, -1), along(values, 2)]


def shards(first_view, second_view, projector):
    clips = first_view.shape[0]
    where = lax.axis_index("row") * 8 + lax.axis_index("col")
    table = lax.dynamic_index_in_dim(jnp.asarray(tables()), where, 0, keepdims=False)

    first_std = reduce_first(*project(table, first_view, projector, FIRST))
    second_std = reduce_second(*project(table, second_view, projector, SECOND))

    columns = fan(jnp.concatenate((first_std, to_near(first_std)), axis=0), along_z)
    turned_high, turned_low, high, low, gram = prepare(table, columns)

    mine = fan(jnp.concatenate((second_std, to_far(second_std)), axis=0), along_x)
    theirs = [to_core(part) for part in mine]

    for move in (to_core, to_first, to_second, to_far):
        gram = gram + move(gram)
    gram = gram[None]
    rows = fan(jnp.concatenate((gram, to_near(gram)), axis=0), along_z)
    grad_two = finish_second(table, rows, first_std, second_std)

    spread = spread_gradient(mine, theirs, high, low)
    parts = lax.all_to_all(spread, "col", 0, 0, tiled=True)
    corr_out = correlate(table, mine, theirs, turned_high, turned_low)
    grad_one = finish_first(parts, first_std, second_std)
    return (
        grad_one.reshape(clips, 1, 1, 128),
        grad_two.reshape(clips, 1, 1, 128),
        corr_out,
    )


def solution(mesh):
    in_specs = (P(None, "row"), P(None, "row"), P("row", "col"))
    out_specs = (
        P(None, "col", "row", None),
        P(None, "col", "row", None),
        P(None, "row", None, "col"),
    )
    return jax.shard_map(shards, mesh=mesh, in_specs=in_specs, out_specs=out_specs, check_vma=False)
```
